32 devices in a mesh: dp: 8 (over z, y), fsdp: 4 (over x, core).
Axes of the slice: x: 2, y: 2, z: 4, core: 2. Of those that a mesh axis runs over, the one named last changes fastest.
Arguments:
- tokens: bfloat16 [1536, 16, 768], P(('dp', 'fsdp')), may hold values from -6 to 6
- image_embed: bfloat16 [1536, 768], P(('dp', 'fsdp')), may hold values from -6 to 6
- counts: int32 [32], replicated, may hold values from 12 to 48, as said below
- end_pos: int32 [1536], P(('dp', 'fsdp')), may hold values from 2 to 15
- ln1_gain: bfloat16 [768], P(('dp', 'fsdp')), may hold values from 0.5 to 1.5
- ln1_bias: bfloat16 [768], P(('dp', 'fsdp')), may hold values from -1.1953125 to 1.1953125
- w_qkv: bfloat16 [768, 2304], P(('dp', 'fsdp')), may hold values from -0.21875 to 0.21875
- w_out: bfloat16 [768, 768], P(('dp', 'fsdp')), may hold values from -0.625 to 0.625
- ln2_gain: bfloat16 [768], P(('dp', 'fsdp')), may hold values from 0.5 to 1.5
- ln2_bias: bfloat16 [768], P(('dp', 'fsdp')), may hold values from -1.1953125 to 1.1953125
- w_up: bfloat16 [768, 3072], P(('dp', 'fsdp')), may hold values from -0.21875 to 0.21875
- b_up: bfloat16 [3072], P(('dp', 'fsdp')), may hold values from -1.1953125 to 1.1953125
- w_down: bfloat16 [3072, 768], P(('dp', 'fsdp')), may hold values from -0.109375 to 0.109375
- b_down: bfloat16 [768], P(('dp', 'fsdp')), may hold values from -1.1953125 to 1.1953125
Outputs:
- mean_loss: float32 [], replicated
- grad_tokens: float32 [1536, 16, 768], P(('dp', 'fsdp'))
- grad_ln1_gain: float32 [768], P(('dp', 'fsdp'))
- grad_ln1_bias: float32 [768], P(('dp', 'fsdp'))
- grad_w_qkv: float32 [768, 2304], P(('dp', 'fsdp'))
- grad_w_out: float32 [768, 768], P(('dp', 'fsdp'))
- grad_ln2_gain: float32 [768], P(('dp', 'fsdp'))
- grad_ln2_bias: float32 [768], P(('dp', 'fsdp'))
- grad_w_up: float32 [768, 3072], P(('dp', 'fsdp'))
- grad_b_up: float32 [3072], P(('dp', 'fsdp'))
- grad_w_down: float32 [3072, 768], P(('dp', 'fsdp'))
- grad_b_down: float32 [768], P(('dp', 'fsdp'))
The draws below stay inside these ranges and needn't reach their ends.
Inputs may be any that keep to these rules, and one draw needn't show every extreme that they name: counts[r] valid captions occupy the first counts[r] of the 48 slots of device r; some device is full in every draw. Slots 0 to end_pos of a caption are its tokens.
All inputs are finite; a program needn't handle non-finite values.
Results may differ from the reference program's by a relative error of at most 0.0109.
Values may be sent and summed in bfloat16 or wider, within the bound.
A program may use at most 192 MiB of HBM per device.

```python
import math
import jax
import jax.numpy as jnp
from jax import lax

D = 768
HEADS = 12
HEAD_DIM = 64
FF = 3072
L = 16
CAP_DEV = 48
RANKS = 32
CAPTIONS = 1536


def draw_counts(key, part):
    key_draw, key_pick = jax.random.split(key)
    drawn_counts = jax.random.randint(key_draw, (RANKS,), max(1, CAP_DEV // 4), CAP_DEV + 1)
    chosen = jax.random.randint(key_pick, (), 0, RANKS)
    return jnp.where(jnp.arange(RANKS) == chosen, CAP_DEV, drawn_counts).astype(jnp.int32)


def touch_ends(drawn, stream_key, smallest, top_value):
    longest = drawn.shape.index(max(drawn.shape))
    spots = []
    for shift in (0, 1):
        where = [jax.random.randint(jax.random.fold_in(stream_key, axis), (), 0, length) for axis, length in enumerate(drawn.shape)]
        where[longest] = (where[longest] + shift) % drawn.shape[longest]
        spots.append(tuple(where))
    return drawn.at[spots[0]].set(smallest).at[spots[1]].set(top_value)


def level_of(stream_key, shape, cuts, smallest, high):
    gain, own = 1.0, jax.random.fold_in(stream_key, 6)
    for position, parts in cuts:
        steps = jnp.exp(jax.random.uniform(jax.random.fold_in(own, position), (parts,), jnp.float32, smallest / len(cuts), high / len(cuts)))
        gain = gain * jnp.repeat(steps, shape[position] // parts).reshape([-1 if axis == position else 1 for axis in range(len(shape))])
    return gain


def bell_draw(key, shape, width, bound, cuts=(), kind=jnp.bfloat16):
    result = width * jax.random.normal(key, shape, jnp.float32)
    if cuts:
        result = result * level_of(key, shape, cuts, -0.22, 0.18)
    return jnp.clip(result, -bound, bound).astype(kind)


def setup_inputs(seed: int = 0) -> dict:
    arg_keys = jax.random.split(jax.random.key(seed), 15)
    return {
        "tokens": bell_draw(arg_keys[0], (CAPTIONS, L, D), 1.0, 6.0, ((0, 32),)),
        "image_embed": bell_draw(arg_keys[1], (CAPTIONS, D), 1.0, 6.0, ((0, 32),)),
        "counts": draw_counts(jax.random.fold_in(arg_keys[14], 71), 0),
        "end_pos": touch_ends(jax.random.randint(arg_keys[3], (CAPTIONS,), 2, L), jax.random.fold_in(arg_keys[3], 1), 2, L - 1).astype(jnp.int32),
        "ln1_gain": jnp.clip(1.0 + 0.1 * jax.random.normal(arg_keys[4], (D,), jnp.float32), 0.5, 1.5).astype(jnp.bfloat16),
        "ln1_bias": bell_draw(arg_keys[5], (D,), 0.2, 1.1953125, ((0, 32),)),
        "w_qkv": bell_draw(arg_keys[6], (D, 3 * D), D ** -0.5, 0.21875, ((0, 32),)),
        "w_out": bell_draw(arg_keys[7], (D, D), (D // 9) ** -0.5, 0.625, ((0, 32),)),
        "ln2_gain": jnp.clip(1.0 + 0.1 * jax.random.normal(arg_keys[8], (D,), jnp.float32), 0.5, 1.5).astype(jnp.bfloat16),
        "ln2_bias": bell_draw(arg_keys[9], (D,), 0.2, 1.1953125, ((0, 32),)),
        "w_up": bell_draw(arg_keys[10], (D, FF), D ** -0.5, 0.21875, ((0, 32),)),
        "b_up": bell_draw(arg_keys[11], (FF,), 0.2, 1.1953125, ((0, 32),)),
        "w_down": bell_draw(arg_keys[12], (FF, D), FF ** -0.5, 0.109375, ((0, 32),)),
        "b_down": bell_draw(arg_keys[13], (D,), 0.2, 1.1953125, ((0, 32),)),
    }


EPS = 1e-05
NORM_EPS = 1e-06
SCALE = 50.0
NEG = -1e+30
HIGHEST_PREC = lax.Precision.HIGHEST

@jax.custom_vjp
def low(v):
    return lax.optimization_barrier(v.astype(jnp.bfloat16)).astype(jnp.float32)

@jax.custom_vjp
def low_back(v):
    return v

def low_keep(v):
    return (low(v), None)

def low_pass(kept, grad):
    return (grad,)

def back_keep(v):
    return (v, None)

def back_low(kept, grad):
    return (low(grad),)
low.defvjp(low_keep, low_pass)
low_back.defvjp(back_keep, back_low)

def layer_norm(values, gain_vec, shift_vec):
    average = lax.optimization_barrier(jnp.mean(values, axis=-1, keepdims=True))
    centred = values - average
    variance = lax.optimization_barrier(jnp.mean(centred * centred, axis=-1, keepdims=True))
    return centred * lax.rsqrt(variance + EPS) * gain_vec + shift_vec

def unit_rows(values):
    return values * lax.rsqrt(lax.optimization_barrier(jnp.sum(values * values, axis=-1, keepdims=True)) + NORM_EPS)

def block_layer(weights, tok_block, end_block):
    ln1_g, ln1_b, wqkv_f, wout_f, ln2_g, ln2_b, wup_f, bup_f, wdown_f, bdown_f = weights
    caps_n = tok_block.shape[0]
    normed = low(layer_norm(tok_block, ln1_g, ln1_b))
    qkv_all = low(low_back(jnp.einsum('cld,de->cle', normed, wqkv_f, precision=HIGHEST_PREC)))
    qkv_all = qkv_all.reshape(caps_n, L, 3, HEADS, HEAD_DIM)
    queries = qkv_all[:, :, 0]
    keys_all = qkv_all[:, :, 1]
    values_all = qkv_all[:, :, 2]
    raw_scores = low_back(jnp.einsum('cqhe,ckhe->chqk', queries, keys_all, precision=HIGHEST_PREC) * HEAD_DIM ** (-0.5))
    positions = jnp.arange(L, dtype=jnp.int32)
    key_ok = positions[None, :] <= end_block[:, None]
    masked = jnp.where(key_ok[:, None, None, :], raw_scores, NEG)
    probs_low = low(jax.nn.softmax(masked, axis=-1))
    mixed_heads = jnp.einsum('chqk,ckhe->cqhe', probs_low, values_all, precision=HIGHEST_PREC)
    mixed_heads = low(low_back(mixed_heads.reshape(caps_n, L, D)))
    branch = low_back(jnp.einsum('cld,de->cle', mixed_heads, wout_f, precision=HIGHEST_PREC))
    hidden1 = tok_block + branch
    normed2 = low(layer_norm(hidden1, ln2_g, ln2_b))
    upper_pre = low_back(jnp.einsum('cld,df->clf', normed2, wup_f, precision=HIGHEST_PREC) + bup_f)
    acted_val = low(jax.nn.gelu(upper_pre, approximate=False))
    output = low_back(jnp.einsum('clf,fd->cld', acted_val, wdown_f, precision=HIGHEST_PREC) + bdown_f)
    hidden2 = hidden1 + output
    end_pick = (positions[None, :] == end_block[:, None]).astype(jnp.float32)
    pooled = lax.optimization_barrier(jnp.sum(hidden2 * end_pick[:, :, None], axis=1))
    return low(unit_rows(pooled))

def reference(tokens, image_embed, counts, end_pos, ln1_gain, ln1_bias, w_qkv, w_out, ln2_gain, ln2_bias, w_up, b_up, w_down, b_down):
    params = tuple((weight_arr.astype(jnp.float32) for weight_arr in (ln1_gain, ln1_bias, w_qkv, w_out, ln2_gain, ln2_bias, w_up, b_up, w_down, b_down)))
    tokens_f = tokens.astype(jnp.float32)
    images_n = low(unit_rows(image_embed.astype(jnp.float32)))
    row_ids = jnp.arange(CAPTIONS, dtype=jnp.int32)
    valid_rows = (row_ids % CAP_DEV < jnp.take(counts, row_ids // CAP_DEV)).astype(jnp.float32)
    group_size = math.gcd(CAPTIONS, 256)
    group_count = CAPTIONS // group_size
    end_groups = end_pos.reshape(group_count, group_size)

    def forward(weights, tok_all):
        tok_groups = tok_all.reshape(group_count, group_size, L, D)

        def scan_step(state_in, pieces):
            return (state_in, jax.checkpoint(block_layer)(weights, pieces[0], pieces[1]))
        unused, text_blocks = lax.scan(scan_step, jnp.zeros((), jnp.float32), (tok_groups, end_groups))
        text_unit = text_blocks.reshape(CAPTIONS, D)
        product = low_back(jnp.dot(text_unit, images_n.T, precision=HIGHEST_PREC))
        logits = SCALE * product
        row_lse = jax.scipy.special.logsumexp(jnp.where(valid_rows[None, :] > 0, logits, NEG), axis=1)
        col_lse = jax.scipy.special.logsumexp(jnp.where(valid_rows[:, None] > 0, logits, NEG), axis=0)
        diagonal = SCALE * lax.optimization_barrier(jnp.sum(text_unit * images_n, axis=1))
        return 0.5 * jnp.sum(valid_rows * (row_lse - diagonal)) + 0.5 * jnp.sum(valid_rows * (col_lse - diagonal))
    objective, pullback = jax.vjp(forward, params, tokens_f)
    grad_params, grad_tok = pullback(jnp.ones_like(objective))
    mean_loss = objective / jnp.sum(valid_rows)
    return (mean_loss, grad_tok, grad_params[0], grad_params[1], grad_params[2], grad_params[3], grad_params[4], grad_params[5], grad_params[6], grad_params[7], grad_params[8], grad_params[9])
```

```python
import jax
import jax.numpy as jnp
from jax import lax
from jax.sharding import PartitionSpec as P

HEAD_DIM = 64
EPS = 1e-05
NORM_EPS = 1e-06
SCALE = 50.0
NEG = -1e30
AXES = ("dp", "fsdp")
F32 = jnp.float32
BF16 = jnp.bfloat16


def norm_stats(values):
    average = jnp.mean(values, axis=-1, keepdims=True)
    centred = values - average
    inverse = lax.rsqrt(jnp.mean(centred * centred, axis=-1, keepdims=True) + EPS)
    return centred * inverse, inverse


def norm_back(d_normed, hat, inverse, gain):
    d_hat = d_normed * gain
    mean_one = jnp.mean(d_hat, axis=-1, keepdims=True)
    mean_two = jnp.mean(d_hat * hat, axis=-1, keepdims=True)
    return inverse * (d_hat - mean_one - hat * mean_two)


def unit_scale(values):
    return lax.rsqrt(jnp.sum(values * values, axis=-1, keepdims=True) + NORM_EPS)


def dot(left, right, dims=((1,), (0,))):
    return lax.dot_general(left, right, (dims, ((), ())), preferred_element_type=F32)


def gelu_and_slope(upper):
    tail = lax.erfc(upper * (-(0.5**0.5)))
    half = 0.5 * tail
    slope = half + upper * jnp.exp(-0.5 * upper * upper) * (0.5 * jnp.pi) ** -0.5 * 0.5
    return upper * half, slope


def gather(value):
    return lax.all_gather(value, AXES, axis=0, tiled=True)


def scatter(value):
    return lax.psum_scatter(value, AXES, scatter_dimension=0, tiled=True)


def on_device(
    tokens,
    image_embed,
    counts,
    end_pos,
    ln1_gain,
    ln1_bias,
    w_qkv,
    w_out,
    ln2_gain,
    ln2_bias,
    w_up,
    b_up,
    w_down,
    b_down,
):
    caps, slots, dim = tokens.shape
    rows = caps * slots
    heads = dim // HEAD_DIM
    me = lax.axis_index(AXES)
    wqkv = gather(w_qkv)
    wout = gather(w_out)
    wup = gather(w_up)
    wdown = gather(w_down)
    small = [gather(v).astype(F32) for v in (ln1_gain, ln1_bias, ln2_gain, ln2_bias, b_up, b_down)]
    gain1, bias1, gain2, bias2, bup, bdown = small
    image = image_embed.astype(F32)
    image_low = (image * unit_scale(image)).astype(BF16)
    image_all = gather(image_low)

    lane_head = lax.broadcasted_iota(jnp.int32, (dim, heads), 0) // HEAD_DIM
    head_of = lax.broadcasted_iota(jnp.int32, (dim, heads), 1)
    pick = (lane_head == head_of).astype(BF16)

    def by_head(product):
        high = product.astype(BF16)
        low = (product - high.astype(F32)).astype(BF16)
        return dot(high, pick) + dot(low, pick)

    def spread(value):
        return dot(value, pick, ((1,), (1,)))

    positions = jnp.arange(slots, dtype=jnp.int32)
    at_end = (positions[None, :] == end_pos[:, None]).astype(F32)[:, :, None]
    counted = (positions[None, :] <= end_pos[:, None])[:, :, None]

    def row_at_end(value):
        return jnp.sum(value.reshape(caps, slots, -1) * at_end, axis=1)

    inputs = tokens.reshape(rows, dim).astype(F32)
    hat1, inverse1 = norm_stats(inputs)
    a1 = (hat1 * gain1 + bias1).astype(BF16)
    a1_end = row_at_end(a1.astype(F32)).astype(BF16)
    inputs_end = row_at_end(inputs)
    query = dot(a1_end, wqkv[:, :dim]).astype(BF16)
    kv = dot(a1, wqkv[:, dim:]).astype(BF16)
    keys = kv[:, :dim].reshape(caps, slots, dim).astype(F32)
    vals = kv[:, dim:].reshape(caps, slots, dim).astype(F32)
    query_f = query.astype(F32)[:, None, :]
    scores = by_head((query_f * keys).reshape(rows, dim)) * HEAD_DIM**-0.5
    scores = jnp.where(counted, scores.reshape(caps, slots, heads), NEG)
    top = jnp.max(scores, axis=1, keepdims=True)
    weight = jnp.exp(scores - top)
    probs = weight / jnp.sum(weight, axis=1, keepdims=True)
    probs_low = probs.astype(BF16)
    probs_wide = spread(probs_low.reshape(rows, heads)).reshape(caps, slots, dim)
    mixed = jnp.sum(probs_wide * vals, axis=1).astype(BF16)
    hidden1 = inputs_end + dot(mixed, wout)
    hat2, inverse2 = norm_stats(hidden1)
    a2 = (hat2 * gain2 + bias2).astype(BF16)
    upper = dot(a2, wup) + bup
    acted, slope = gelu_and_slope(upper)
    acted_low = acted.astype(BF16)
    pooled = hidden1 + dot(acted_low, wdown) + bdown
    scale_t = unit_scale(pooled)
    unit = pooled * scale_t
    text_low = unit.astype(BF16)
    own_image = image_low.astype(F32)
    diagonal = SCALE * jnp.sum(text_low.astype(F32) * own_image, axis=1)

    total = caps * counts.shape[0]
    slot_of = lax.broadcasted_iota(jnp.int32, (counts.shape[0], caps), 1)
    valid_all = (slot_of < counts[:, None]).astype(F32).reshape(total)
    own_count = jnp.sum(jnp.where(jnp.arange(counts.shape[0]) == me, counts, 0))
    own_valid = (jnp.arange(caps) < own_count).astype(F32)
    growth = jnp.exp(SCALE * dot(text_low, image_all, ((1,), (1,))))
    row_sum = jnp.sum(growth * valid_all[None, :], axis=1)
    col_sum = lax.psum(jnp.sum(growth * own_valid[:, None], axis=0), AXES)
    row_part = jnp.sum(own_valid * (0.5 * jnp.log(row_sum) - diagonal))
    objective = lax.psum(row_part, AXES) + 0.5 * jnp.sum(valid_all * jnp.log(col_sum))
    mean_loss = objective / jnp.sum(counts).astype(F32)
    inverse_sum = 1.0 / row_sum[:, None] + 1.0 / col_sum[None, :]
    coef = 0.5 * SCALE * growth * inverse_sum * (own_valid[:, None] * valid_all[None, :])
    d_text = dot(coef.astype(BF16), image_all) - SCALE * own_valid[:, None] * own_image
    d_pooled = (d_text - unit * jnp.sum(unit * d_text, axis=-1, keepdims=True)) * scale_t

    dm = d_pooled.astype(BF16)
    g_wdown = dot(acted_low, dm, ((0,), (0,)))
    g_bdown = jnp.sum(dm.astype(F32), axis=0)
    du = (dot(dm, wdown, ((1,), (1,))) * slope).astype(BF16)
    g_bup = jnp.sum(du.astype(F32), axis=0)
    g_wup = dot(a2, du, ((0,), (0,)))
    d_a2 = dot(du, wup, ((1,), (1,)))
    g_gain2 = jnp.sum(d_a2 * hat2, axis=0)
    g_bias2 = jnp.sum(d_a2, axis=0)
    d_hidden1 = d_pooled + norm_back(d_a2, hat2, inverse2, gain2)
    da = d_hidden1.astype(BF16)
    g_wout = dot(mixed, da, ((0,), (0,)))
    d_mixed = dot(da, wout, ((1,), (1,))).astype(BF16).astype(F32)[:, None, :]
    d_vals = probs_wide * d_mixed
    d_probs = by_head((vals * d_mixed).reshape(rows, dim)).reshape(caps, slots, heads)
    d_scores = probs * (d_probs - jnp.sum(d_probs * probs, axis=1, keepdims=True))
    d_wide = spread(d_scores.astype(BF16).reshape(rows, heads)).reshape(caps, slots, dim)
    d_query = (HEAD_DIM**-0.5 * jnp.sum(d_wide * keys, axis=1)).astype(BF16)
    d_keys = HEAD_DIM**-0.5 * d_wide * query_f
    d_kv = jnp.concatenate([d_keys, d_vals], axis=-1).reshape(rows, 2 * dim).astype(BF16)
    g_wqkv = jnp.concatenate(
        [dot(a1_end, d_query, ((0,), (0,))), dot(a1, d_kv, ((0,), (0,)))], axis=1
    )
    d_a1_end = dot(d_query, wqkv[:, :dim], ((1,), (1,)))
    d_a1 = dot(d_kv, wqkv[:, dim:], ((1,), (1,)))
    d_a1 = d_a1 + (d_a1_end[:, None, :] * at_end).reshape(rows, dim)
    g_gain1 = jnp.sum(d_a1 * hat1, axis=0)
    g_bias1 = jnp.sum(d_a1, axis=0)
    grad_tokens = norm_back(d_a1, hat1, inverse1, gain1).reshape(caps, slots, dim)
    grad_tokens = grad_tokens + at_end * d_hidden1[:, None, :]
    return (
        mean_loss,
        grad_tokens,
        scatter(g_gain1),
        scatter(g_bias1),
        scatter(g_wqkv),
        scatter(g_wout),
        scatter(g_gain2),
        scatter(g_bias2),
        scatter(g_wup),
        scatter(g_bup),
        scatter(g_wdown),
        scatter(g_bdown),
    )


def solution(mesh):
    one, two, three = P(AXES), P(AXES, None), P(AXES, None, None)
    placed = (three, two, P(), one, one, one, two, two, one, one, two, one, two, one)
    given = (P(), three, one, one, two, two, one, one, two, one, two, one)
    return jax.shard_map(
        on_device, mesh=mesh, in_specs=placed, out_specs=given, check_vma=False
    )
```
